256 devices in a mesh: slab: 32 (over z, x), freq: 8 (over y, core).
Axes of the slice: x: 4, y: 4, z: 8, core: 2. Of those that a mesh axis runs over, the one named last changes fastest.
Arguments:
- wavefield: float32 [2, 96, 32, 32768], P(None, 'freq', None, 'slab'), may hold values from -6 to 6
- observed: float32 [2, 96, 32, 16384], P(None, None, 'freq', 'slab'), may hold values from -6 to 6
- filters: float32 [32, 256], P('freq'), may hold values from -0.375 to 0.375
- mute: int32 [32, 16384], P('freq', 'slab'), may hold values from 0 to 511
- send_cell: int32 [32, 1024], P('slab'), may hold values from 0 to 1023, as said below
- send_count: int32 [32, 32], P('slab'), may hold values from 0 to 32, as said below
- recv_pos: int32 [32, 1024], P('slab'), may hold values from -1 to 511, as said below
Outputs:
- adjoint: float32 [2, 96, 32, 32768], P(None, 'freq', None, 'slab')
The draws below stay inside these ranges and needn't reach their ends.
Inputs may be any that keep to these rules, and one draw needn't show every extreme that they name: `send_cell`: row s lists distinct cells of slab s; slots at or beyond send_count[s, d] hold cells too and carry no receiver. `send_count`: for every trace group d the column d sums to 512, and its largest entry is 32. `recv_pos`: entry s * 32 + k of row d is the trace's place in group d when k < send_count[s, d], else -1; the places of one row are each of 0 to 511 once.
All inputs are finite; a program needn't handle non-finite values.
Results may differ from the reference program's by a relative error of at most 0.0003.
Values sent between devices are 32-bit elements; how exact they have to be, the bound alone decides.
No kernel may reach another device: no remote copies, remote signals or barrier semaphores. Data moves between devices by JAX's collectives and lax.ppermute only.
A program may use at most 128 MiB of HBM per device.

```python
import math
import jax
import jax.numpy as jnp
from jax import lax

F = 96
NT = 1024
TAPS = 256
K0 = 8
SHOTS = 32
CELLS = 1024
TR_SLAB = 512
TRACES = 16384
SLOT = 32
CELLS_ALL = 32768
N_SLAB = 32


def shuffled_sources(key):
    return jax.random.permutation(key, N_SLAB)


def shuffled_cells(key):
    return jax.random.permutation(key, CELLS)[:N_SLAB * SLOT]


def shuffled_places(key):
    return jax.random.permutation(key, TR_SLAB)


def pair_lists(key):
    halfway = SLOT // 2
    subkeys = jax.random.split(key, 4)
    orders = jax.vmap(shuffled_sources)(jax.random.split(subkeys[0], N_SLAB))
    shifts = jax.random.randint(subkeys[1], (N_SLAB, N_SLAB // 2), 0, halfway + 1)
    shifts = shifts.at[:, 0].set(halfway)
    firsts = orders[:, 0::2]
    seconds = orders[:, 1::2]
    row_ids = jnp.arange(N_SLAB, dtype=jnp.int32)[:, None]
    by_group = jnp.zeros((N_SLAB, N_SLAB), jnp.int32)
    by_group = by_group.at[row_ids, firsts].set(halfway + shifts)
    by_group = by_group.at[row_ids, seconds].set(halfway - shifts)
    counts = jnp.transpose(by_group)
    cells = jax.vmap(shuffled_cells)(jax.random.split(subkeys[2], N_SLAB))
    places = jax.vmap(shuffled_places)(jax.random.split(subkeys[3], N_SLAB))
    offsets = jnp.cumsum(by_group, axis=1) - by_group
    slot_ids = jnp.arange(SLOT, dtype=jnp.int32)
    ranks = offsets[:, :, None] + slot_ids[None, None, :]
    living = slot_ids[None, None, :] < by_group[:, :, None]
    picked = jnp.take_along_axis(places, jnp.clip(ranks, 0, TR_SLAB - 1).reshape(N_SLAB, N_SLAB * SLOT), axis=1)
    positions = jnp.where(living.reshape(N_SLAB, N_SLAB * SLOT), picked, -1)
    return (counts.astype(jnp.int32), cells.astype(jnp.int32), positions.astype(jnp.int32))


def draw_send_cell(key, part):
    return pair_lists(jax.random.fold_in(key, 31))[1]


def draw_send_count(key, part):
    return pair_lists(jax.random.fold_in(key, 31))[0]


def draw_recv_pos(key, part):
    return pair_lists(jax.random.fold_in(key, 31))[2]


def plant(drawn, own_key, smallest, high):
    dims = drawn.shape
    index_at = [jax.random.randint(jax.random.fold_in(own_key, axis), (), 0, dims[axis]) for axis in range(len(dims))]
    drawn = drawn.at[tuple(index_at)].set(smallest)
    longest = dims.index(max(dims))
    index_at[longest] = (index_at[longest] + 1) % dims[longest]
    return drawn.at[tuple(index_at)].set(high)


def level_of(stream_key, extent, cuts, low, largest):
    def one(dim, parts):
        steps = jax.random.uniform(jax.random.fold_in(jax.random.fold_in(stream_key, 6), dim), (parts,), jnp.float32, low / len(cuts), largest / len(cuts))
        return jnp.repeat(jnp.exp(steps), extent[dim] // parts).reshape((-1,) + (1,) * (len(extent) - dim - 1))

    level = one(*cuts[0])
    for cut in cuts[1:]:
        level = level * one(*cut)
    return level


def gaussian(own_key, extent, deviation, limit, cuts=(), kind=jnp.bfloat16):
    loudness = level_of(own_key, extent, cuts, -0.22, 0.18) if cuts else 1.0
    values = jax.random.normal(own_key, extent, jnp.float32) * deviation * loudness
    return jnp.minimum(jnp.maximum(values, -limit), limit).astype(kind)


def setup_inputs(seed: int = 0) -> dict:
    streams_of = jax.random.split(jax.random.key(seed), 8)
    return {
        "wavefield": gaussian(streams_of[0], (2, F, SHOTS, CELLS_ALL), 1.0, 6.0, ((1, 8), (3, 32)), jnp.float32),
        "observed": gaussian(streams_of[1], (2, F, SHOTS, TRACES), 1.0, 6.0, ((2, 8), (3, 32)), jnp.float32),
        "filters": gaussian(streams_of[2], (SHOTS, TAPS), TAPS ** -0.5, 0.375, ((0, 8),), jnp.float32),
        "mute": plant(jax.random.randint(streams_of[3], (SHOTS, TRACES), 0, NT // 2), jax.random.fold_in(streams_of[3], 1), 0, (NT // 2) - 1).astype(jnp.int32),
        "send_cell": draw_send_cell(jax.random.fold_in(streams_of[7], 71), 0),
        "send_count": draw_send_count(jax.random.fold_in(streams_of[7], 71), 0),
        "recv_pos": draw_recv_pos(jax.random.fold_in(streams_of[7], 71), 0),
    }


def tables():
    bins_used = K0 + jnp.arange(F, dtype=jnp.int32)
    sample_ids = jnp.arange(NT, dtype=jnp.int32)
    phases = bins_used[:, None] * sample_ids[None, :] % NT
    angles = phases.astype(jnp.float32) * (2.0 * math.pi / NT)
    cosine = jnp.cos(angles)
    sine_part = jnp.sin(angles)
    inverse = jnp.stack([cosine, -sine_part]) / math.sqrt(F)
    forward = jnp.stack([cosine, -sine_part]) / math.sqrt(NT)
    return (inverse, forward)

def toeplitz(filter_taps):
    column = jnp.arange(TAPS, dtype=jnp.int32)
    offset = column[None, :] - column[:, None]
    lower = jnp.where(offset >= 0, filter_taps[jnp.clip(offset, 0, TAPS - 1)], 0.0)
    upper = jnp.where(offset < 0, filter_taps[jnp.clip(offset + TAPS, 0, TAPS - 1)], 0.0)
    return (lower, upper)

def apply_filter(traces, lower, upper):
    shaped = traces.reshape(traces.shape[:-1] + (NT // TAPS, TAPS))
    earlier = jnp.concatenate([jnp.zeros_like(shaped[..., :1, :]), shaped[..., :-1, :]], axis=-2)
    result = jnp.einsum('tbi,ij->tbj', shaped, lower, precision=lax.Precision.HIGHEST)
    result = result + jnp.einsum('tbi,ij->tbj', earlier, upper, precision=lax.Precision.HIGHEST)
    return result.reshape(traces.shape)

def reference(wavefield, observed, filters, mute, send_cell, send_count, recv_pos):
    slot_rows = send_cell.shape[1] // N_SLAB
    all_traces = observed.shape[3]
    group_traces = all_traces // N_SLAB
    cells_dev = wavefield.shape[3] // N_SLAB
    groups = jnp.arange(N_SLAB, dtype=jnp.int32)
    slot_ids = jnp.arange(slot_rows, dtype=jnp.int32)
    live = slot_ids[None, None, :] < send_count[:, :, None]
    global_cell = groups[:, None, None] * cells_dev + send_cell.reshape(N_SLAB, N_SLAB, slot_rows)
    places = jnp.transpose(recv_pos.reshape(N_SLAB, N_SLAB, slot_rows), (1, 0, 2))
    global_trace = groups[None, :, None] * group_traces + places
    global_trace = jnp.where(live, global_trace, all_traces).astype(jnp.int32)
    cell_flat = global_cell.reshape(-1).astype(jnp.int32)
    trace_flat = global_trace.reshape(-1)
    live_flat = live.reshape(-1)
    predicted = jnp.zeros(observed.shape, jnp.float32).at[..., trace_flat].set(wavefield[..., cell_flat], mode='drop')
    inverse, forward = tables()

    def one_shot(items):
        spectrum, filter_taps, cutoff, measured = items
        traces = jnp.einsum('cft,cfn->tn', spectrum, inverse, precision=lax.Precision.HIGHEST)
        lower, upper = toeplitz(filter_taps)
        filtered = apply_filter(traces, lower, upper)
        keeper = jnp.arange(NT, dtype=jnp.int32)[None, :] >= cutoff[:, None]
        filtered = jnp.where(keeper, filtered, 0.0)
        return jnp.einsum('tn,cfn->cft', filtered, forward, precision=lax.Precision.HIGHEST) - measured
    residual = lax.map(one_shot, (jnp.moveaxis(predicted, 2, 0), filters, mute, jnp.moveaxis(observed, 2, 0)))
    residual = jnp.moveaxis(residual, 0, 2)
    picked = residual[..., jnp.clip(trace_flat, 0, all_traces - 1)]
    picked = jnp.where(live_flat, picked, 0.0)
    return jnp.zeros_like(wavefield).at[..., cell_flat].add(picked)
```

```python
import functools
import math

import jax
import jax.numpy as jnp
from jax import lax
from jax.experimental import pallas as pl
from jax.experimental.pallas import tpu as pltpu
from jax.sharding import PartitionSpec as P

F = 96
NT = 1024
TAPS = 256
K0 = 8
HALF = 512
NF = 8
FB = F // NF
ROWS = 2 * FB
CF = 2 * F
SLABS = 32
SLOT = 32
NSH = 4
VMEM = 60 << 20
BF = jnp.bfloat16
F32 = jnp.float32


def split(x):
    hi = x.astype(BF)
    return hi, (x - hi.astype(F32)).astype(BF)


def mm(a, b):
    return jnp.dot(a, b, preferred_element_type=F32)


def call(kernel, outs, n_in, *, smem=(), scratch=(), flops=0, nbytes=0):
    specs = [
        pl.BlockSpec(memory_space=pltpu.SMEM if i in smem else pltpu.VMEM) for i in range(n_in)
    ]
    vm = pl.BlockSpec(memory_space=pltpu.VMEM)
    return pl.pallas_call(
        kernel,
        out_shape=outs,
        in_specs=specs,
        out_specs=[vm] * len(outs),
        scratch_shapes=list(scratch),
        compiler_params=pltpu.CompilerParams(vmem_limit_bytes=VMEM),
        cost_estimate=pl.CostEstimate(flops=flops, bytes_accessed=nbytes, transcendentals=0),
    )


def sds(*shape, dtype=F32):
    return jax.ShapeDtypeStruct(shape, dtype)


def tables():
    row = jnp.arange(CF, dtype=jnp.int32)
    part = (row % ROWS) // FB
    freq = K0 + (row // ROWS) * FB + row % FB
    t = jnp.arange(NT, dtype=jnp.int32)

    def wave(f, c, t):
        angle = (f * t % NT).astype(F32) * (2.0 * math.pi / NT)
        return jnp.where(c == 0, jnp.cos(angle), -jnp.sin(angle))

    forward = wave(freq[:, None], part[:, None], t[None, :]) / math.sqrt(NT)
    inverse_t = wave(freq[None, :], part[None, :], t[:, None]) / math.sqrt(F)
    return forward, inverse_t


def operator_kernel(taps_ref, fwd_ref, inv_ref, gh_ref, gl_ref, bh_ref, bl_ref, g_ref):
    late = fwd_ref[:, HALF:]
    for n in range(NSH):
        rows = jnp.broadcast_to(taps_ref[n : n + 1, :], (TAPS, 2 * TAPS))
        band = pltpu.roll(rows, 1, 1, stride=1, stride_axis=0)
        for b in range(NT // TAPS):
            if b == 0:
                g = jnp.dot(band[:, TAPS:], inv_ref[:TAPS, :], precision=lax.Precision.HIGHEST)
            else:
                g = jnp.dot(
                    band,
                    inv_ref[(b - 1) * TAPS : (b + 1) * TAPS, :],
                    precision=lax.Precision.HIGHEST,
                )
            if b < 2:
                hi, lo = split(g)
                gh_ref[n, b * TAPS : (b + 1) * TAPS, :] = hi
                gl_ref[n, b * TAPS : (b + 1) * TAPS, :] = lo
            else:
                g_ref[(b - 2) * TAPS : (b - 1) * TAPS, :] = g
        hi, lo = split(jnp.dot(late, g_ref[...], precision=lax.Precision.HIGHEST))
        bh_ref[n] = hi
        bl_ref[n] = lo


def pack_kernel(obs_ref, pos_ref, mute_ref, out_ref, ms_ref, y_ref):
    group = obs_ref.shape[2]
    slots = pos_ref.shape[1]
    pick = (
        lax.broadcasted_iota(jnp.int32, (group, slots), 0) == jnp.broadcast_to(pos_ref[...], (group, slots))
    ).astype(F32).astype(BF)
    mh, ml = split(mute_ref[...].astype(F32))
    ms_ref[...] = mm(mh, pick) + mm(ml, pick)
    for n in range(NSH):
        hi, lo = split(obs_ref[n])
        y_ref[n] = mm(hi, pick) + mm(lo, pick)
    lane = lax.broadcasted_iota(jnp.int32, (CF, 128), 1) // SLOT
    for tile in range(SLABS // 4):
        parts = [y_ref[n, :, tile * 128 : (tile + 1) * 128] for n in range(NSH)]
        for b in range(4):
            acc = None
            for n in range(NSH):
                shift = ((n - b) % 4) * SLOT
                v = pltpu.roll(parts[n], shift, 1) if shift else parts[n]
                acc = v if acc is None else jnp.where(lane == n, v, acc)
            out_ref[4 * tile + b] = acc.reshape(NF, ROWS, 128)


def route_kernel(me_ref, x_ref, *refs):
    outs, st_ref = refs[:NF], refs[NF]
    for o in range(4):
        st_ref[8 * o : 8 * o + 8] = jnp.swapaxes(x_ref[:, 8 * o : 8 * o + 8, :], 0, 1)
    me = me_ref[0]
    for k in range(NF):
        j = lax.rem(me + k, NF)
        outs[k][...] = st_ref[pl.ds(j * NSH, NSH)]


def place_kernel(cell_ref, ms_ref, hot_ref, mc_ref):
    slots = cell_ref.shape[0]
    cells = hot_ref.shape[1]
    hot = (
        lax.broadcasted_iota(jnp.int32, (slots, cells), 1) == jnp.broadcast_to(cell_ref[...], (slots, cells))
    ).astype(F32).astype(BF)
    hot_ref[...] = hot
    hi, lo = split(ms_ref[...])
    mc_ref[...] = mm(hi, hot) + mm(lo, hot)


def trace_kernel(me_ref, *refs):
    xs = refs[:NF]
    gh_ref, gl_ref, bh_ref, bl_ref, fwd_ref, mc_ref = refs[NF : NF + 6]
    outs = refs[NF + 6 : 2 * NF + 6]
    fh_ref, fl_ref, x_ref, r_ref = refs[2 * NF + 6 :]
    me = me_ref[0]
    fh, fl = split(fwd_ref[:, :HALF])
    fh_ref[...] = fh
    fl_ref[...] = fl
    cells = x_ref.shape[1]
    width = 256
    t = lax.broadcasted_iota(jnp.int32, (HALF, width), 0).astype(F32)

    @pl.loop(0, NSH)
    def _(n):
        for k in range(NF):
            j = lax.rem(me - k + NF, NF)
            x_ref[pl.ds(pl.multiple_of(j * ROWS, 8), ROWS), :] = xs[k][n]
        for w in range(cells // width):
            at = slice(w * width, (w + 1) * width)
            live = mc_ref[NSH : NSH + 1, at]
            x = jnp.where(live > 0.5, x_ref[:, at], 0.0)
            xh, xl = split(x)
            gh = gh_ref[n]
            y = mm(gh, xh) + mm(gh, xl) + mm(gl_ref[n], xh)
            cut = mc_ref[pl.ds(n, 1), at]
            y = jnp.where(t >= cut, y, 0.0)
            yh, yl = split(y)
            bh = bh_ref[n]
            r = mm(fh_ref[...], yh) + mm(fh_ref[...], yl) + mm(fl_ref[...], yh)
            r = r + mm(bh, xh) + mm(bh, xl) + mm(bl_ref[n], xh)
            r_ref[:, at] = r
        for k in range(NF):
            j = lax.rem(me + k, NF)
            outs[k][n] = r_ref[pl.ds(pl.multiple_of(j * ROWS, 8), ROWS), :]


def finish_kernel(me_ref, z_ref, hot_ref, *refs):
    rs = refs[:NF]
    out_ref = refs[NF]
    a_ref, p_ref, s_ref = refs[NF + 1 :]
    me = me_ref[0]
    lane = lax.broadcasted_iota(jnp.int32, (NF, ROWS, 128), 2) // SLOT
    for n in range(NSH):
        for tile in range(SLABS // 4):
            acc = None
            for e in range(4):
                shift = ((e - n) % 4) * SLOT
                v = z_ref[4 * tile + e]
                if shift:
                    v = pltpu.roll(v, shift, 2)
                acc = v if acc is None else jnp.where(lane == e, v, acc)
            a_ref[:, tile * 128 : (tile + 1) * 128] = acc.reshape(CF, 128)
        hi, lo = split(a_ref[...])
        p_ref[...] = mm(hi, hot_ref[...]) + mm(lo, hot_ref[...])
        for k in range(NF):
            j = lax.rem(me - k + NF, NF)
            s_ref[j * NSH + n] = rs[k][n] - p_ref[pl.ds(pl.multiple_of(j * ROWS, 8), ROWS), :]
    for o in range(4):
        out_ref[:, 8 * o : 8 * o + 8, :] = jnp.swapaxes(s_ref[8 * o : 8 * o + 8], 0, 1)


def shift_by(values, k):
    return lax.ppermute(values, "freq", [(i, (i + k) % NF) for i in range(NF)])


def on_device(wavefield, observed, filters, mute, send_cell, send_count, recv_pos):
    cells = wavefield.shape[3]
    group = observed.shape[3]
    slots = send_cell.shape[1]
    slab = lax.axis_index("slab")
    me = lax.axis_index("freq").astype(jnp.int32).reshape(1)

    obs = observed.reshape(2, NF, FB, NSH, group).transpose(3, 1, 0, 2, 4).reshape(NSH, CF, group)
    packed, mute_slots = call(
        pack_kernel,
        [sds(SLABS, NF, ROWS, 128), sds(NSH, slots)],
        3,
        scratch=[pltpu.VMEM((NSH, CF, slots), F32)],
        flops=2 * 2 * NSH * CF * group * slots,
        nbytes=4 * NSH * CF * (group + slots),
    )(obs, recv_pos, mute)
    packed = packed.reshape(SLABS * NF, ROWS, 128)
    arrived = lax.all_to_all(packed, ("slab", "freq"), split_axis=0, concat_axis=0, tiled=True)
    arrived = arrived.reshape(SLABS, NF, ROWS, 128)
    mute_all = lax.all_gather(mute_slots, "slab")

    blocks = call(
        route_kernel,
        [sds(NSH, ROWS, cells)] * NF,
        2,
        smem=(0,),
        scratch=[pltpu.VMEM((NSH * NF, ROWS, cells), F32)],
        nbytes=8 * NSH * CF * cells,
    )(me, wavefield.reshape(ROWS, NSH * NF, cells))
    spectra = [blocks[0]] + [shift_by(blocks[k], k) for k in range(1, NF)]

    forward, inverse_t = tables()
    taps = jnp.concatenate([filters[:, ::-1], jnp.zeros_like(filters)], axis=1)
    gh, gl, bh, bl = call(
        operator_kernel,
        [sds(NSH, HALF, CF, dtype=BF)] * 2 + [sds(NSH, CF, CF, dtype=BF)] * 2,
        3,
        scratch=[pltpu.VMEM((HALF, CF), F32)],
        flops=6 * 2 * NSH * CF * (1024 * 512 + CF * HALF),
        nbytes=1 << 22,
    )(taps, forward, inverse_t)

    live = jnp.arange(SLOT, dtype=jnp.int32)[None, :] < send_count[0][:, None]
    target = jnp.where(live.reshape(-1), send_cell[0], -1).reshape(slots, 1)
    mine = lax.dynamic_slice(mute_all, (0, 0, slab * SLOT), (SLABS, NSH, SLOT))
    mine = mine.transpose(1, 0, 2).reshape(NSH, slots)
    mine = jnp.concatenate([mine, jnp.ones((NSH, slots), F32)], axis=0)
    hot, at_cells = call(
        place_kernel,
        [sds(slots, cells, dtype=BF), sds(2 * NSH, cells)],
        2,
        flops=4 * 8 * slots * cells,
        nbytes=2 * slots * cells,
    )(target, mine)

    results = call(
        trace_kernel,
        [sds(NSH, ROWS, cells)] * NF,
        NF + 7,
        smem=(0,),
        scratch=[
            pltpu.VMEM((CF, HALF), BF),
            pltpu.VMEM((CF, HALF), BF),
            pltpu.VMEM((CF, cells), F32),
            pltpu.VMEM((CF, cells), F32),
        ],
        flops=6 * NSH * cells * (2 * CF * HALF + CF * CF),
        nbytes=8 * NSH * CF * cells,
    )(me, *spectra, gh, gl, bh, bl, forward, at_cells)
    returned = [results[0]] + [shift_by(results[k], k) for k in range(1, NF)]

    (out,) = call(
        finish_kernel,
        [sds(ROWS, NSH * NF, cells)],
        NF + 3,
        smem=(0,),
        scratch=[
            pltpu.VMEM((CF, slots), F32),
            pltpu.VMEM((CF, cells), F32),
            pltpu.VMEM((NSH * NF, ROWS, cells), F32),
        ],
        flops=4 * NSH * CF * slots * cells,
        nbytes=12 * NSH * CF * cells,
    )(me, arrived, hot, *returned)
    return out.reshape(2, FB, NSH * NF, cells)


def solution(mesh):
    return jax.shard_map(
        on_device,
        mesh=mesh,
        in_specs=(
            P(None, "freq", None, "slab"),
            P(None, None, "freq", "slab"),
            P("freq", None),
            P("freq", "slab"),
            P("slab", None),
            P("slab", None),
            P("slab", None),
        ),
        out_specs=P(None, "freq", None, "slab"),
        check_vma=False,
    )
```

```python
import functools
import math

import jax
import jax.numpy as jnp
from jax import lax
from jax.experimental import pallas as pl
from jax.experimental.pallas import tpu as pltpu
from jax.sharding import PartitionSpec as P

F = 96
NT = 1024
TAPS = 256
K0 = 8
HALF = 512
NF = 8
FB = F // NF
ROWS = 2 * FB
CF = 2 * F
SLABS = 32
SLOT = 32
NSH = 4
VMEM = 60 << 20
BF = jnp.bfloat16
F32 = jnp.float32


def split(x):
    hi = x.astype(BF)
    return hi, (x - hi.astype(F32)).astype(BF)


def mm(a, b):
    return jnp.dot(a, b, preferred_element_type=F32)


def call(kernel, outs, n_in, *, smem=(), scratch=(), flops=0, nbytes=0):
    specs = [
        pl.BlockSpec(memory_space=pltpu.SMEM if i in smem else pltpu.VMEM) for i in range(n_in)
    ]
    vm = pl.BlockSpec(memory_space=pltpu.VMEM)
    return pl.pallas_call(
        kernel,
        out_shape=outs,
        in_specs=specs,
        out_specs=[vm] * len(outs),
        scratch_shapes=list(scratch),
        compiler_params=pltpu.CompilerParams(vmem_limit_bytes=VMEM),
        cost_estimate=pl.CostEstimate(flops=flops, bytes_accessed=nbytes, transcendentals=0),
    )


def sds(*shape, dtype=F32):
    return jax.ShapeDtypeStruct(shape, dtype)


def tables():
    row = jnp.arange(CF, dtype=jnp.int32)
    part = (row % ROWS) // FB
    freq = K0 + (row // ROWS) * FB + row % FB
    t = jnp.arange(NT, dtype=jnp.int32)

    def wave(f, c, t):
        angle = (f * t % NT).astype(F32) * (2.0 * math.pi / NT)
        return jnp.where(c == 0, jnp.cos(angle), -jnp.sin(angle))

    forward = wave(freq[:, None], part[:, None], t[None, :]) / math.sqrt(NT)
    inverse_t = wave(freq[None, :], part[None, :], t[:, None]) / math.sqrt(F)
    return forward, inverse_t


def operator_kernel(taps_ref, fwd_ref, inv_ref, hi_ref, lo_ref, g_ref):
    late = fwd_ref[:, HALF:]
    for n in range(NSH):
        rows = jnp.broadcast_to(taps_ref[n : n + 1, :], (TAPS, 2 * TAPS))
        band = pltpu.roll(rows, 1, 1, stride=1, stride_axis=0)
        for b in range(NT // TAPS):
            if b == 0:
                g = jnp.dot(band[:, TAPS:], inv_ref[:TAPS, :], precision=lax.Precision.HIGHEST)
            else:
                g = jnp.dot(
                    band,
                    inv_ref[(b - 1) * TAPS : (b + 1) * TAPS, :],
                    precision=lax.Precision.HIGHEST,
                )
            if b < 2:
                hi, lo = split(g)
                hi_ref[n, b * TAPS : (b + 1) * TAPS, :] = hi
                lo_ref[n, b * TAPS : (b + 1) * TAPS, :] = lo
            else:
                g_ref[(b - 2) * TAPS : (b - 1) * TAPS, :] = g
        hi, lo = split(jnp.dot(late, g_ref[...], precision=lax.Precision.HIGHEST))
        hi_ref[n, HALF:, :] = hi
        lo_ref[n, HALF:, :] = lo


def mute_kernel(pos_ref, mute_ref, ms_ref):
    group = mute_ref.shape[1]
    slots = pos_ref.shape[1]
    pick = (
        lax.broadcasted_iota(jnp.int32, (group, slots), 0) == jnp.broadcast_to(pos_ref[...], (group, slots))
    ).astype(F32).astype(BF)
    mh, ml = split(mute_ref[...].astype(F32))
    ms_ref[...] = mm(mh, pick) + mm(ml, pick)


def pack_kernel(me_ref, pos_ref, *refs):
    blocks = refs[:NF]
    out_ref, x_ref, y_ref = refs[NF:]
    me = me_ref[0]
    group = x_ref.shape[2]
    slots = pos_ref.shape[1]
    part = CF
    for k in range(NF):
        x_ref[:, k * NSH : (k + 1) * NSH, :] = blocks[k][...]
    pick = (
        lax.broadcasted_iota(jnp.int32, (group, slots), 0) == jnp.broadcast_to(pos_ref[...], (group, slots))
    ).astype(F32).astype(BF)
    each = ROWS // 4
    for g in range(4):
        x = pltpu.roll(x_ref[g * each : (g + 1) * each], me * NSH, 1)
        hi, lo = split(x.reshape(part, group))
        y_ref[g] = mm(hi, pick) + mm(lo, pick)
    lane = lax.broadcasted_iota(jnp.int32, (part, 128), 1) // SLOT
    for tile in range(SLABS // 4):
        parts = [y_ref[g, :, tile * 128 : (tile + 1) * 128] for g in range(4)]
        for b in range(4):
            acc = None
            for g in range(4):
                shift = ((g - b) % 4) * SLOT
                v = pltpu.roll(parts[g], shift, 1) if shift else parts[g]
                acc = v if acc is None else jnp.where(lane == g, v, acc)
            out_ref[4 * tile + b] = acc


def route_kernel(me_ref, x_ref, *refs):
    outs, st_ref = refs[:NF], refs[NF]
    for o in range(4):
        st_ref[8 * o : 8 * o + 8] = jnp.swapaxes(x_ref[:, 8 * o : 8 * o + 8, :], 0, 1)
    me = me_ref[0]
    for k in range(NF):
        j = lax.rem(me + k, NF)
        outs[k][...] = st_ref[pl.ds(j * NSH, NSH)]


def place_kernel(cell_ref, ms_ref, hot_ref, mc_ref):
    slots = cell_ref.shape[0]
    cells = hot_ref.shape[1]
    hot = (
        lax.broadcasted_iota(jnp.int32, (slots, cells), 1) == jnp.broadcast_to(cell_ref[...], (slots, cells))
    ).astype(F32).astype(BF)
    hot_ref[...] = hot
    hi, lo = split(ms_ref[...])
    mc_ref[...] = mm(hi, hot) + mm(lo, hot)


def trace_kernel(me_ref, *refs):
    xs = refs[:NF]
    hi_ref, lo_ref, fwd_ref, mc_ref = refs[NF : NF + 4]
    outs = refs[NF + 4 : 2 * NF + 4]
    f_ref, x_ref, r_ref = refs[2 * NF + 4 :]
    me = me_ref[0]
    fh, fl = split(fwd_ref[:, :HALF])
    f_ref[:CF] = fh
    f_ref[CF:] = fl
    cells = x_ref.shape[1]
    width = 256
    t = lax.broadcasted_iota(jnp.int32, (HALF, width), 0).astype(F32)

    @pl.loop(0, NSH)
    def _(n):
        for k in range(NF):
            j = lax.rem(me - k + NF, NF)
            x_ref[pl.ds(pl.multiple_of(j * ROWS, 8), ROWS), :] = xs[k][n]
        for w in range(cells // width):
            at = slice(w * width, (w + 1) * width)
            live = mc_ref[NSH : NSH + 1, at]
            x = jnp.where(live > 0.5, x_ref[:, at], 0.0)
            xh, xl = split(x)
            table = hi_ref[n]
            u = mm(table, xh)
            v = mm(lo_ref[n], xh)
            z = mm(table, xl)
            cut = mc_ref[pl.ds(n, 1), at]
            y = jnp.where(t >= cut, u[:HALF] + v[:HALF] + z[:HALF], 0.0)
            r = u[HALF:] + v[HALF:] + z[HALF:]
            yh, yl = split(y)
            p = mm(f_ref[...], yh)
            r = r + p[:CF] + p[CF:] + mm(f_ref[:CF], yl)
            r_ref[:, at] = r
        for k in range(NF):
            j = lax.rem(me + k, NF)
            outs[k][n] = r_ref[pl.ds(pl.multiple_of(j * ROWS, 8), ROWS), :]


def finish_kernel(me_ref, z_ref, hot_ref, *refs):
    rs = refs[:NF]
    out_ref = refs[NF]
    a_ref, s_ref = refs[NF + 1 :]
    me = me_ref[0]
    for k in range(NF):
        j = lax.rem(me - k + NF, NF)
        s_ref[pl.ds(j * NSH, NSH)] = rs[k][...]
    for o in range(4):
        out_ref[:, 8 * o : 8 * o + 8, :] = jnp.swapaxes(s_ref[8 * o : 8 * o + 8], 0, 1)
    lane = lax.broadcasted_iota(jnp.int32, (CF, 128), 1) // SLOT
    each = ROWS // 4
    for g in range(4):
        for tile in range(SLABS // 4):
            acc = None
            for e in range(4):
                shift = ((e - g) % 4) * SLOT
                v = z_ref[4 * tile + e]
                if shift:
                    v = pltpu.roll(v, shift, 1)
                acc = v if acc is None else jnp.where(lane == e, v, acc)
            a_ref[:, tile * 128 : (tile + 1) * 128] = acc
        hi, lo = split(a_ref[...])
        p = mm(hi, hot_ref[...]) + mm(lo, hot_ref[...])
        at = slice(g * each, (g + 1) * each)
        out_ref[at] = out_ref[at] - p.reshape(each, NSH * NF, p.shape[1])


def shift_by(values, k):
    return lax.ppermute(values, "freq", [(i, (i + k) % NF) for i in range(NF)])


def on_device(wavefield, observed, filters, mute, send_cell, send_count, recv_pos):
    cells = wavefield.shape[3]
    group = observed.shape[3]
    slots = send_cell.shape[1]
    me = lax.axis_index("freq").astype(jnp.int32).reshape(1)

    (mute_slots,) = call(mute_kernel, [sds(NSH, slots)], 2, flops=1 << 26, nbytes=1 << 16)(
        recv_pos, mute
    )
    mute_slots = mute_slots.reshape(NSH, SLABS, SLOT).transpose(1, 0, 2).reshape(SLABS, 1, 128)
    mine = lax.all_to_all(mute_slots, "slab", split_axis=0, concat_axis=0, tiled=True)
    obs = observed.reshape(2, NF, FB, NSH, group)
    own = [
        lax.dynamic_index_in_dim(obs, lax.rem(me[0] + NF - k, NF), 1, keepdims=False).reshape(
            ROWS, NSH, group
        )
        for k in range(NF)
    ]
    own = [own[0]] + [shift_by(own[k], NF - k) for k in range(1, NF)]
    (packed,) = call(
        pack_kernel,
        [sds(SLABS, CF, 128)],
        NF + 2,
        smem=(0,),
        scratch=[pltpu.VMEM((ROWS, NSH * NF, group), F32), pltpu.VMEM((4, CF, slots), F32)],
        flops=2 * 2 * NSH * CF * group * slots,
        nbytes=4 * NSH * CF * (group + slots),
    )(me, recv_pos, *own)
    arrived = lax.all_to_all(packed, "slab", split_axis=0, concat_axis=0, tiled=True)

    blocks = call(
        route_kernel,
        [sds(NSH, ROWS, cells)] * NF,
        2,
        smem=(0,),
        scratch=[pltpu.VMEM((NSH * NF, ROWS, cells), F32)],
        nbytes=8 * NSH * CF * cells,
    )(me, wavefield.reshape(ROWS, NSH * NF, cells))
    spectra = [blocks[0]] + [shift_by(blocks[k], k) for k in range(1, NF)]

    forward, inverse_t = tables()
    taps = jnp.concatenate([filters[:, ::-1], jnp.zeros_like(filters)], axis=1)
    hi, lo = call(
        operator_kernel,
        [sds(NSH, HALF + CF, CF, dtype=BF)] * 2,
        3,
        scratch=[pltpu.VMEM((HALF, CF), F32)],
        flops=6 * 2 * NSH * CF * (1024 * 512 + CF * HALF),
        nbytes=1 << 22,
    )(taps, forward, inverse_t)

    live = jnp.arange(SLOT, dtype=jnp.int32)[None, :] < send_count[0][:, None]
    target = jnp.where(live.reshape(-1), send_cell[0], -1).reshape(slots, 1)
    mine = mine.reshape(SLABS, NSH, SLOT).transpose(1, 0, 2).reshape(NSH, slots)
    mine = jnp.concatenate([mine, jnp.ones((NSH, slots), F32)], axis=0)
    hot, at_cells = call(
        place_kernel,
        [sds(slots, cells, dtype=BF), sds(2 * NSH, cells)],
        2,
        flops=4 * 8 * slots * cells,
        nbytes=2 * slots * cells,
    )(target, mine)

    results = call(
        trace_kernel,
        [sds(NSH, ROWS, cells)] * NF,
        NF + 5,
        smem=(0,),
        scratch=[
            pltpu.VMEM((2 * CF, HALF), BF),
            pltpu.VMEM((CF, cells), F32),
            pltpu.VMEM((CF, cells), F32),
        ],
        flops=6 * NSH * cells * (2 * CF * HALF + CF * CF),
        nbytes=8 * NSH * CF * cells,
    )(me, *spectra, hi, lo, forward, at_cells)
    returned = [results[0]] + [shift_by(results[k], k) for k in range(1, NF)]

    (out,) = call(
        finish_kernel,
        [sds(ROWS, NSH * NF, cells)],
        NF + 3,
        smem=(0,),
        scratch=[
            pltpu.VMEM((CF, slots), F32),
            pltpu.VMEM((NSH * NF, ROWS, cells), F32),
        ],
        flops=4 * NSH * CF * slots * cells,
        nbytes=12 * NSH * CF * cells,
    )(me, arrived, hot, *returned)
    return out.reshape(2, FB, NSH * NF, cells)


def solution(mesh):
    return jax.shard_map(
        on_device,
        mesh=mesh,
        in_specs=(
            P(None, "freq", None, "slab"),
            P(None, None, "freq", "slab"),
            P("freq", None),
            P("freq", "slab"),
            P("slab", None),
            P("slab", None),
            P("slab", None),
        ),
        out_specs=P(None, "freq", None, "slab"),
        check_vma=False,
    )
```

```python
import math

import jax
import jax.numpy as jnp
import numpy as np
from jax import lax
from jax.experimental import pallas as pl
from jax.experimental.pallas import tpu as pltpu
from jax.sharding import PartitionSpec as P

F = 96
NT = 1024
TAPS = 256
K0 = 8
HALF = 512
NF = 8
FB = F // NF
ROWS = 2 * FB
CF = 2 * F
SLABS = 32
SLOT = 32
MAIN = 768
NSH = 4
VMEM = 28 << 20
COST = pl.CostEstimate(flops=1000, bytes_accessed=1000, transcendentals=0)
WIDTH = 512
WIDE = 1024
HBM = pl.BlockSpec(memory_space=pltpu.HBM)
INV = pl.BlockSpec(memory_space=pltpu.VMEM)
INS = pl.BlockSpec(memory_space=pltpu.SMEM)
BF = jnp.bfloat16
F32 = jnp.float32


def split(x):
    hi = x.astype(BF)
    return hi, (x - hi.astype(F32)).astype(BF)


def mm(a, b):
    return jnp.dot(a, b, preferred_element_type=F32)


def regroup(parts, at, lane):
    acc = None
    for m in range(4):
        shift = (m - at) % 4 * SLOT
        v = pltpu.roll(parts[m], shift, parts[m].ndim - 1) if shift else parts[m]
        acc = v if acc is None else jnp.where(lane == m, v, acc)
    return acc


def mt(a, b):
    return lax.dot_general(a, b, (((1,), (1,)), ((), ())), preferred_element_type=F32)


def call(kernel, outs, n_in, *, smem=(), scratch=(), vmem=VMEM):
    specs = [
        pl.BlockSpec(memory_space=pltpu.SMEM if i in smem else pltpu.VMEM) for i in range(n_in)
    ]
    vm = pl.BlockSpec(memory_space=pltpu.VMEM)
    return pl.pallas_call(
        kernel,
        out_shape=outs,
        in_specs=specs,
        out_specs=[vm] * len(outs),
        scratch_shapes=list(scratch),
        compiler_params=pltpu.CompilerParams(vmem_limit_bytes=vmem),
        cost_estimate=COST,
    )


def copy_call(kernel, outs, in_specs, scratch, vmem=60 << 20):
    return pl.pallas_call(
        kernel,
        out_shape=outs,
        in_specs=in_specs,
        out_specs=[HBM] * len(outs),
        scratch_shapes=list(scratch),
        compiler_params=pltpu.CompilerParams(vmem_limit_bytes=vmem),
        cost_estimate=COST,
    )


def grid_call(kernel, outs, in_specs, out_specs, scratch):
    return pl.pallas_call(
        kernel,
        grid=(4,),
        out_shape=outs,
        in_specs=in_specs,
        out_specs=out_specs,
        scratch_shapes=list(scratch),
        compiler_params=pltpu.CompilerParams(vmem_limit_bytes=VMEM),
        cost_estimate=COST,
    )


def sds(*shape, dtype=F32):
    return jax.ShapeDtypeStruct(shape, dtype)


def forward_table():
    row = np.arange(CF)
    part = (row % ROWS) // FB
    freq = K0 + (row // ROWS) * FB + row % FB
    angle = (freq[:, None] * np.arange(NT)[None, :] % NT) * (2.0 * math.pi / NT)
    wave = np.where(part[:, None] == 0, np.cos(angle), -np.sin(angle))
    return (wave / math.sqrt(NT)).astype(np.float32)


def operator_kernel(taps_ref, fwd_ref, hi_ref, lo_ref, ih_ref, il_ref, g_ref):
    ih, il = split(fwd_ref[...] * math.sqrt(NT / F))
    ih_ref[...] = ih
    il_ref[...] = il
    late = split(fwd_ref[:, HALF:])

    @pl.loop(0, NSH)
    def _(n):
        rows = jnp.broadcast_to(taps_ref[pl.ds(n, 1), :], (TAPS, 2 * TAPS))
        bh, bl = split(pltpu.roll(rows, 1, 1, stride=1, stride_axis=0))
        for b in range(NT // TAPS):
            at = slice(max(b - 1, 0) * TAPS, (b + 1) * TAPS)
            taps = slice(TAPS if b == 0 else 0, 2 * TAPS)
            g = mt(bh[:, taps], ih_ref[:, at]) + mt(bh[:, taps], il_ref[:, at])
            g = g + mt(bl[:, taps], ih_ref[:, at])
            if b < 2:
                hi, lo = split(g)
                hi_ref[n, b * TAPS : (b + 1) * TAPS, :] = hi
                lo_ref[n, b * TAPS : (b + 1) * TAPS, :] = lo
            else:
                g_ref[(b - 2) * TAPS : (b - 1) * TAPS, :] = g
        gh, gl = split(g_ref[...])
        hi, lo = split(mm(late[0], gh) + mm(late[0], gl) + mm(late[1], gh))
        hi_ref[n, HALF:, :] = hi
        lo_ref[n, HALF:, :] = lo


def mute_kernel(pos_ref, mute_ref, out_ref):
    group = mute_ref.shape[1]
    slots = pos_ref.shape[1]
    pick = (
        lax.broadcasted_iota(jnp.int32, (group, slots), 0) == jnp.broadcast_to(pos_ref[...], (group, slots))
    ).astype(F32).astype(BF)
    mh, ml = split(mute_ref[...].astype(F32))
    got = mm(mh, pick) + mm(ml, pick)
    lane = lax.broadcasted_iota(jnp.int32, (8, 128), 1) // SLOT
    for tile in range(SLABS // 4):
        rows = [
            jnp.broadcast_to(got[n : n + 1, tile * 128 : (tile + 1) * 128], (8, 128))
            for n in range(NSH)
        ]
        for b in range(4):
            out_ref[4 * tile + b] = regroup(rows, b, lane)


def pack_kernel(me_ref, pos_ref, *refs):
    blocks = refs[:NF]
    out_ref, x_ref, h_ref = refs[NF:]
    me = me_ref[0]
    group = x_ref.shape[2]
    slots = pos_ref.shape[1]
    rows = 4 * CF
    for k in range(NF):
        x_ref[:, k * NSH : (k + 1) * NSH, :] = blocks[k][...]
    x = pltpu.roll(x_ref[...], me * NSH, 1).reshape(rows, group)
    h_ref[:rows], h_ref[rows:] = split(x)
    lane = lax.broadcasted_iota(jnp.int32, (CF, 128), 1) // SLOT
    for w in range(slots // WIDTH):
        at = slice(w * WIDTH, (w + 1) * WIDTH)
        pick = (
            lax.broadcasted_iota(jnp.int32, (group, WIDTH), 0)
            == jnp.broadcast_to(pos_ref[:, at], (group, WIDTH))
        ).astype(F32).astype(BF)
        y = mm(h_ref[...], pick)
        y = y[:rows] + y[rows:]
        for i in range(WIDTH // 128):
            tile = w * (WIDTH // 128) + i
            parts = [y[g * CF : (g + 1) * CF, i * 128 : (i + 1) * 128] for g in range(4)]
            for b in range(4):
                out_ref[4 * tile + b] = regroup(parts, b, lane)


def index_kernel(cell_ref, hot_ref, front_ref, back_ref):
    slots, cells = hot_ref.shape
    hot = (
        lax.broadcasted_iota(jnp.int32, (slots, cells), 1) == jnp.broadcast_to(cell_ref[...], (slots, cells))
    ).astype(F32).astype(BF)
    hot_ref[...] = hot
    live = mm(jnp.ones((8, slots), BF), hot)
    before = (
        lax.broadcasted_iota(jnp.int32, (cells, cells), 0) < lax.broadcasted_iota(jnp.int32, (cells, cells), 1)
    ).astype(F32).astype(BF)
    rank = mm(live.astype(BF), before)
    place = jnp.where(live > 0.5, rank, -1.0)[:1]
    back = (
        lax.broadcasted_iota(jnp.int32, (cells, cells), 0).astype(F32) == jnp.broadcast_to(place, (cells, cells))
    ).astype(F32)
    back_ref[...] = back.astype(BF)
    front_ref[...] = jnp.transpose(back).astype(BF)


def route_kernel(me_ref, x_ref, front_ref, *refs):
    outs, rest_ref, st_ref, h_ref = refs[:NF], refs[NF], refs[NF + 1], refs[NF + 2]
    rows, cells = ROWS * NSH * NF, x_ref.shape[2]
    h_ref[:rows], h_ref[rows:] = split(x_ref[...].reshape(rows, cells))

    @pl.loop(0, cells // WIDE)
    def _(w):
        at = pl.ds(pl.multiple_of(w * WIDE, WIDE), WIDE)
        y = mm(h_ref[...], front_ref[:, at])
        y = (y[:rows] + y[rows:]).reshape(ROWS, NSH * NF, WIDE)
        for o in range(4):
            st_ref[8 * o : 8 * o + 8, :, at] = jnp.swapaxes(y[:, 8 * o : 8 * o + 8, :], 0, 1)
    me = me_ref[0]
    for k in range(NF):
        j = lax.rem(me + k, NF)
        outs[k][...] = st_ref[pl.ds(j * NSH, NSH), :, :MAIN]
        rest_ref[k] = st_ref[pl.ds(j * NSH, NSH), :, MAIN:]


def place_kernel(all_ref, hot_ref, front_ref, mc_ref, ms_ref):
    lane = lax.broadcasted_iota(jnp.int32, (8, 128), 1) // SLOT
    ms_ref[...] = jnp.ones_like(ms_ref)
    for tile in range(SLABS // 4):
        for n in range(NSH):
            row = regroup([all_ref[4 * tile + e] for e in range(4)], n, lane)
            ms_ref[n : n + 1, tile * 128 : (tile + 1) * 128] = row[:1]
    hi, lo = split(ms_ref[...])
    hi, lo = split(mm(hi, hot_ref[...]) + mm(lo, hot_ref[...]))
    mc_ref[...] = mm(hi, front_ref[...]) + mm(lo, front_ref[...])


def trace_kernel(me_ref, *refs):
    xs = refs[:NF]
    hi_ref, lo_ref, fwd_ref, mc_ref = refs[NF : NF + 4]
    outs = refs[NF + 4 : 2 * NF + 4]
    f_ref, x_ref, r_ref = refs[2 * NF + 4 :]
    me = me_ref[0]
    n = pl.program_id(0)

    @pl.when(n == 0)
    def _():
        fh, fl = split(fwd_ref[...])
        f_ref[:CF] = fh
        f_ref[CF:] = fl

    for k in range(NF):
        j = lax.rem(me - k + NF, NF)
        x_ref[pl.ds(pl.multiple_of(j * ROWS, 8), ROWS), :] = xs[k][0]
    cells = x_ref.shape[1]
    width = min(MAIN, cells)
    t = lax.broadcasted_iota(jnp.int32, (HALF, width), 0).astype(F32)
    for w in range(cells // width):
        at = slice(w * width, (w + 1) * width)
        live = mc_ref[NSH : NSH + 1, at]
        xh, xl = split(jnp.where(live > 0.5, x_ref[:, at], 0.0))
        table = hi_ref[0]
        u = mm(table, xh) + mm(lo_ref[0], xh) + mm(table, xl)
        cut = mc_ref[pl.ds(n, 1), at]
        yh, yl = split(jnp.where(t >= cut, u[:HALF], 0.0))
        p = mm(f_ref[...], yh)
        r_ref[:, at] = u[HALF:] + p[:CF] + p[CF:] + mm(f_ref[:CF], yl)
    for k in range(NF):
        j = lax.rem(me + k, NF)
        outs[k][0] = r_ref[pl.ds(pl.multiple_of(j * ROWS, 8), ROWS), :]


def turn_kernel(me_ref, back_ref, rest_ref, *refs):
    rs, out_ref, s_ref, h_ref = refs[:NF], refs[NF], refs[NF + 1], refs[NF + 2]
    rows, cells = ROWS * NSH * NF, out_ref.shape[2]
    me = me_ref[0]
    for k in range(NF):
        j = lax.rem(me - k + NF, NF)
        s_ref[pl.ds(j * NSH, NSH), :, :MAIN] = rs[k][...]
        s_ref[pl.ds(j * NSH, NSH), :, MAIN:] = rest_ref[k]
    for o in range(4):
        out_ref[:, 8 * o : 8 * o + 8, :] = jnp.swapaxes(s_ref[8 * o : 8 * o + 8], 0, 1)
    h_ref[:rows], h_ref[rows:] = split(out_ref[...].reshape(rows, cells))

    @pl.loop(0, cells // WIDE)
    def _(w):
        at = pl.ds(pl.multiple_of(w * WIDE, WIDE), WIDE)
        y = mm(h_ref[...], back_ref[:, at])
        out_ref[:, :, at] = (y[:rows] + y[rows:]).reshape(ROWS, NSH * NF, WIDE)


def finish_kernel(z_ref, hot_ref, wave_ref, out_ref, zv_ref, hv_ref, t_ref, h_ref, sem, z_sem, out_sem):
    tiles = SLABS // 4
    z_in = []
    for tile in range(tiles):
        at = slice(4 * tile, 4 * tile + 4)
        z_in.append(pltpu.make_async_copy(z_ref.at[at], zv_ref.at[at], z_sem.at[tile]))
        z_in[tile].start()
    hot_in = pltpu.make_async_copy(hot_ref, hv_ref, sem.at[0])
    hot_in.start()
    wave_in = pltpu.make_async_copy(wave_ref, t_ref, sem.at[1])
    wave_in.start()
    lane = lax.broadcasted_iota(jnp.int32, (CF, 128), 1) // SLOT
    rows = 4 * CF
    for tile in range(tiles):
        z_in[tile].wait()
        parts = [zv_ref[4 * tile + e] for e in range(4)]
        at = slice(tile * 128, (tile + 1) * 128)
        for g in range(4):
            hi, lo = split(regroup(parts, g, lane))
            h_ref[g * CF : (g + 1) * CF, at] = hi
            h_ref[rows + g * CF : rows + (g + 1) * CF, at] = lo
    hot_in.wait()
    wave_in.wait()
    stores = []
    for w in range(t_ref.shape[2] // WIDTH):
        at = slice(w * WIDTH, (w + 1) * WIDTH)
        p = mm(h_ref[...], hv_ref[:, at])
        t_ref[:, :, at] = t_ref[:, :, at] - (p[:rows] + p[rows:]).reshape(ROWS, NSH * NF, WIDTH)
        stores.append(pltpu.make_async_copy(t_ref.at[:, :, at], out_ref.at[:, :, at], out_sem.at[w]))
        stores[w].start()
    for store in stores:
        store.wait()


def shift_by(values, k):
    return lax.ppermute(values, "freq", [(i, (i + k) % NF) for i in range(NF)])


def on_device(wavefield, observed, filters, mute, send_cell, send_count, recv_pos):
    cells = wavefield.shape[3]
    group = observed.shape[3]
    slots = send_cell.shape[1]
    me = lax.axis_index("freq").astype(jnp.int32).reshape(1)

    (mute_slots,) = call(mute_kernel, [sds(SLABS, 8, 128)], 2)(recv_pos, mute)
    mute_all = lax.all_to_all(mute_slots, "slab", split_axis=0, concat_axis=0, tiled=True)
    obs = observed.reshape(2, NF, FB, NSH, group)
    own = [
        lax.dynamic_index_in_dim(obs, lax.rem(me[0] + NF - k, NF), 1, keepdims=False).reshape(
            ROWS, NSH, group
        )
        for k in range(NF)
    ]
    own = [own[0]] + [shift_by(own[k], NF - k) for k in range(1, NF)]
    forward = jnp.asarray(forward_table())
    taps = jnp.concatenate([filters[:, ::-1], jnp.zeros_like(filters)], axis=1)
    hi, lo = call(
        operator_kernel,
        [sds(NSH, HALF + CF, CF, dtype=BF)] * 2,
        2,
        scratch=[pltpu.VMEM((CF, NT), BF), pltpu.VMEM((CF, NT), BF), pltpu.VMEM((HALF, CF), F32)],
    )(taps, forward)
    live = jnp.arange(SLOT, dtype=jnp.int32)[None, :] < send_count[0][:, None]
    target = jnp.where(live.reshape(-1), send_cell[0], -1).reshape(slots, 1)
    hot, front, back = call(
        index_kernel,
        [sds(slots, cells, dtype=BF), sds(cells, cells, dtype=BF), sds(cells, cells, dtype=BF)],
        1,
        vmem=60 << 20,
    )(target)
    *blocks, rest = call(
        route_kernel,
        [sds(NSH, ROWS, MAIN)] * NF + [sds(NF, NSH, ROWS, cells - MAIN)],
        3,
        smem=(0,),
        scratch=[
            pltpu.VMEM((NSH * NF, ROWS, cells), F32),
            pltpu.VMEM((2 * ROWS * NSH * NF, cells), BF),
        ],
        vmem=60 << 20,
    )(me, wavefield.reshape(ROWS, NSH * NF, cells), front)
    own, blocks, rest = lax.optimization_barrier((own, blocks, rest))
    (packed,) = call(
        pack_kernel,
        [sds(SLABS, CF, 128)],
        NF + 2,
        smem=(0,),
        scratch=[
            pltpu.VMEM((ROWS, NSH * NF, group), F32),
            pltpu.VMEM((8 * CF, group), BF),
        ],
    )(me, recv_pos, *own)
    arrived = lax.all_to_all(packed, "slab", split_axis=0, concat_axis=0, tiled=True)


    (at_columns,) = call(
        place_kernel,
        [sds(2 * NSH, cells)],
        3,
        scratch=[pltpu.VMEM((2 * NSH, slots), F32)],
    )(mute_all, hot, front)

    def exchanged(blocks):
        return [blocks[0]] + [shift_by(blocks[k], k) for k in range(1, NF)]

    def traced(blocks, hi, lo, forward, columns):
        width = columns.shape[1]
        block = pl.BlockSpec((1, ROWS, width), lambda n: (n, 0, 0))
        table = pl.BlockSpec((1, HALF + CF, CF), lambda n: (n, 0, 0))
        return grid_call(
            trace_kernel,
            [sds(NSH, ROWS, width)] * NF,
            [INS]
            + [block] * NF
            + [table] * 2
            + [
                pl.BlockSpec((CF, HALF), lambda n: (0, 0)),
                pl.BlockSpec((2 * NSH, width), lambda n: (0, 0)),
            ],
            [block] * NF,
            [
                pltpu.VMEM((2 * CF, HALF), BF),
                pltpu.VMEM((CF, width), F32),
                pltpu.VMEM((CF, width), F32),
            ],
        )(me, *exchanged(blocks), hi, lo, forward, columns)

    def traced_rest(rest, hi, lo, forward, columns):
        parts = [rest[k] for k in range(NF)]
        return jnp.stack(exchanged(traced(parts, hi, lo, forward, columns)))

    main = traced(blocks, hi, lo, forward, at_columns[:, :MAIN])
    main, rest = lax.optimization_barrier((main, rest))
    returned = exchanged(main)
    rest = lax.cond(
        jnp.sum(send_count) > MAIN,
        traced_rest,
        lambda rest, *_: jnp.zeros_like(rest),
        rest,
        hi,
        lo,
        forward,
        at_columns[:, MAIN:],
    )
    (turned,) = call(
        turn_kernel,
        [sds(ROWS, NSH * NF, cells)],
        NF + 3,
        smem=(0,),
        scratch=[
            pltpu.VMEM((NSH * NF, ROWS, cells), F32),
            pltpu.VMEM((2 * ROWS * NSH * NF, cells), BF),
        ],
        vmem=60 << 20,
    )(me, back, rest, *returned)
    dma = pltpu.SemaphoreType.DMA
    (out,) = copy_call(
        finish_kernel,
        [sds(ROWS, NSH * NF, cells)],
        [HBM] * 3,
        [
            pltpu.VMEM((SLABS, CF, 128), F32),
            pltpu.VMEM((slots, cells), BF),
            pltpu.VMEM((ROWS, NSH * NF, cells), F32),
            pltpu.VMEM((8 * CF, slots), BF),
            dma((2,)),
            dma((SLABS // 4,)),
            dma((cells // WIDTH,)),
        ],
    )(arrived, hot, turned)
    return out.reshape(2, FB, NSH * NF, cells)


def solution(mesh):
    return jax.shard_map(
        on_device,
        mesh=mesh,
        in_specs=(
            P(None, "freq", None, "slab"),
            P(None, None, "freq", "slab"),
            P("freq", None),
            P("freq", "slab"),
            P("slab", None),
            P("slab", None),
            P("slab", None),
        ),
        out_specs=P(None, "freq", None, "slab"),
        check_vma=False,
    )
```

```python
import math

import jax
import jax.numpy as jnp
import numpy as np
from jax import lax
from jax.experimental import pallas as pl
from jax.experimental.pallas import tpu as pltpu
from jax.sharding import PartitionSpec as P

F = 96
NT = 1024
TAPS = 256
K0 = 8
HALF = 512
NF = 8
FB = F // NF
ROWS = 2 * FB
CF = 2 * F
SLABS = 32
SLOT = 32
MAIN = 768
NSH = 4
VMEM = 28 << 20
COST = pl.CostEstimate(flops=1000, bytes_accessed=1000, transcendentals=0)
WIDTH = 512
WIDE = 1024
HBM = pl.BlockSpec(memory_space=pltpu.HBM)
INV = pl.BlockSpec(memory_space=pltpu.VMEM)
INS = pl.BlockSpec(memory_space=pltpu.SMEM)
BF = jnp.bfloat16
F32 = jnp.float32


def split(x):
    hi = x.astype(BF)
    return hi, (x - hi.astype(F32)).astype(BF)


def mm(a, b):
    return jnp.dot(a, b, preferred_element_type=F32)


def regroup(parts, at, lane):
    acc = None
    for m in range(4):
        shift = (m - at) % 4 * SLOT
        v = pltpu.roll(parts[m], shift, parts[m].ndim - 1) if shift else parts[m]
        acc = v if acc is None else jnp.where(lane == m, v, acc)
    return acc


def mt(a, b):
    return lax.dot_general(a, b, (((1,), (1,)), ((), ())), preferred_element_type=F32)


def call(kernel, outs, n_in, *, smem=(), scratch=(), vmem=VMEM):
    specs = [
        pl.BlockSpec(memory_space=pltpu.SMEM if i in smem else pltpu.VMEM) for i in range(n_in)
    ]
    vm = pl.BlockSpec(memory_space=pltpu.VMEM)
    return pl.pallas_call(
        kernel,
        out_shape=outs,
        in_specs=specs,
        out_specs=[vm] * len(outs),
        scratch_shapes=list(scratch),
        compiler_params=pltpu.CompilerParams(vmem_limit_bytes=vmem),
        cost_estimate=COST,
    )


def copy_call(kernel, outs, in_specs, scratch, vmem=60 << 20):
    return pl.pallas_call(
        kernel,
        out_shape=outs,
        in_specs=in_specs,
        out_specs=[HBM] * len(outs),
        scratch_shapes=list(scratch),
        compiler_params=pltpu.CompilerParams(vmem_limit_bytes=vmem),
        cost_estimate=COST,
    )


def grid_call(kernel, outs, in_specs, out_specs, scratch):
    return pl.pallas_call(
        kernel,
        grid=(4,),
        out_shape=outs,
        in_specs=in_specs,
        out_specs=out_specs,
        scratch_shapes=list(scratch),
        compiler_params=pltpu.CompilerParams(vmem_limit_bytes=VMEM),
        cost_estimate=COST,
    )


def sds(*shape, dtype=F32):
    return jax.ShapeDtypeStruct(shape, dtype)


def forward_table():
    row = np.arange(CF)
    part = (row % ROWS) // FB
    freq = K0 + (row // ROWS) * FB + row % FB
    angle = (freq[:, None] * np.arange(NT)[None, :] % NT) * (2.0 * math.pi / NT)
    wave = np.where(part[:, None] == 0, np.cos(angle), -np.sin(angle))
    return (wave / math.sqrt(NT)).astype(np.float32)


def operator_kernel(taps_ref, fwd_ref, hi_ref, lo_ref, ih_ref, il_ref, g_ref):
    ih, il = split(fwd_ref[...] * math.sqrt(NT / F))
    ih_ref[...] = ih
    il_ref[...] = il
    late = split(fwd_ref[:, HALF:])

    @pl.loop(0, NSH)
    def _(n):
        rows = jnp.broadcast_to(taps_ref[pl.ds(n, 1), :], (TAPS, 2 * TAPS))
        bh, bl = split(pltpu.roll(rows, 1, 1, stride=1, stride_axis=0))
        for b in range(NT // TAPS):
            at = slice(max(b - 1, 0) * TAPS, (b + 1) * TAPS)
            taps = slice(TAPS if b == 0 else 0, 2 * TAPS)
            g = mt(bh[:, taps], ih_ref[:, at]) + mt(bh[:, taps], il_ref[:, at])
            g = g + mt(bl[:, taps], ih_ref[:, at])
            if b < 2:
                hi, lo = split(g)
                hi_ref[n, b * TAPS : (b + 1) * TAPS, :] = hi
                lo_ref[n, b * TAPS : (b + 1) * TAPS, :] = lo
            else:
                g_ref[(b - 2) * TAPS : (b - 1) * TAPS, :] = g
        gh, gl = split(g_ref[...])
        hi, lo = split(mm(late[0], gh) + mm(late[0], gl) + mm(late[1], gh))
        hi_ref[n, HALF:, :] = hi
        lo_ref[n, HALF:, :] = lo


def mute_kernel(pos_ref, mute_ref, out_ref):
    group = mute_ref.shape[1]
    slots = pos_ref.shape[1]
    pick = (
        lax.broadcasted_iota(jnp.int32, (group, slots), 0) == jnp.broadcast_to(pos_ref[...], (group, slots))
    ).astype(F32).astype(BF)
    mh, ml = split(mute_ref[...].astype(F32))
    got = mm(mh, pick) + mm(ml, pick)
    lane = lax.broadcasted_iota(jnp.int32, (8, 128), 1) // SLOT
    for tile in range(SLABS // 4):
        rows = [
            jnp.broadcast_to(got[n : n + 1, tile * 128 : (tile + 1) * 128], (8, 128))
            for n in range(NSH)
        ]
        for b in range(4):
            out_ref[4 * tile + b] = regroup(rows, b, lane)


def pack_kernel(me_ref, pos_ref, *refs):
    blocks = refs[:NF]
    out_ref, x_ref, h_ref = refs[NF:]
    me = me_ref[0]
    group = x_ref.shape[2]
    slots = pos_ref.shape[1]
    rows = 4 * CF
    for k in range(NF):
        x_ref[:, k * NSH : (k + 1) * NSH, :] = blocks[k][...]
    x = pltpu.roll(x_ref[...], me * NSH, 1).reshape(rows, group)
    h_ref[:rows], h_ref[rows:] = split(x)
    lane = lax.broadcasted_iota(jnp.int32, (CF, 128), 1) // SLOT
    for w in range(slots // WIDTH):
        at = slice(w * WIDTH, (w + 1) * WIDTH)
        pick = (
            lax.broadcasted_iota(jnp.int32, (group, WIDTH), 0)
            == jnp.broadcast_to(pos_ref[:, at], (group, WIDTH))
        ).astype(F32).astype(BF)
        y = mm(h_ref[...], pick)
        y = y[:rows] + y[rows:]
        for i in range(WIDTH // 128):
            tile = w * (WIDTH // 128) + i
            parts = [y[g * CF : (g + 1) * CF, i * 128 : (i + 1) * 128] for g in range(4)]
            for b in range(4):
                out_ref[4 * tile + b] = regroup(parts, b, lane)


def index_kernel(cell_ref, hot_ref, front_ref, back_ref):
    slots, cells = hot_ref.shape
    hot = (
        lax.broadcasted_iota(jnp.int32, (slots, cells), 1) == jnp.broadcast_to(cell_ref[...], (slots, cells))
    ).astype(F32).astype(BF)
    hot_ref[...] = hot
    live = mm(jnp.ones((8, slots), BF), hot)
    before = (
        lax.broadcasted_iota(jnp.int32, (cells, cells), 0) < lax.broadcasted_iota(jnp.int32, (cells, cells), 1)
    ).astype(F32).astype(BF)
    rank = mm(live.astype(BF), before)
    place = jnp.where(live > 0.5, rank, -1.0)[:1]
    back = (
        lax.broadcasted_iota(jnp.int32, (cells, cells), 0).astype(F32) == jnp.broadcast_to(place, (cells, cells))
    ).astype(F32)
    back_ref[...] = back.astype(BF)
    front_ref[...] = jnp.transpose(back).astype(BF)


def route_kernel(me_ref, x_ref, front_ref, *refs):
    outs, rest_ref, st_ref, h_ref = refs[:NF], refs[NF], refs[NF + 1], refs[NF + 2]
    rows, cells = ROWS * NSH * NF, x_ref.shape[2]
    h_ref[:rows], h_ref[rows:] = split(x_ref[...].reshape(rows, cells))

    @pl.loop(0, cells // WIDE)
    def _(w):
        at = pl.ds(pl.multiple_of(w * WIDE, WIDE), WIDE)
        y = mm(h_ref[...], front_ref[:, at])
        y = (y[:rows] + y[rows:]).reshape(ROWS, NSH * NF, WIDE)
        for o in range(4):
            st_ref[8 * o : 8 * o + 8, :, at] = jnp.swapaxes(y[:, 8 * o : 8 * o + 8, :], 0, 1)
    me = me_ref[0]
    for k in range(NF):
        j = lax.rem(me + k, NF)
        outs[k][...] = st_ref[pl.ds(j * NSH, NSH), :, :MAIN]
        rest_ref[k] = st_ref[pl.ds(j * NSH, NSH), :, MAIN:]


def place_kernel(all_ref, hot_ref, front_ref, mc_ref, ms_ref):
    lane = lax.broadcasted_iota(jnp.int32, (8, 128), 1) // SLOT
    ms_ref[...] = jnp.ones_like(ms_ref)
    for tile in range(SLABS // 4):
        for n in range(NSH):
            row = regroup([all_ref[4 * tile + e] for e in range(4)], n, lane)
            ms_ref[n : n + 1, tile * 128 : (tile + 1) * 128] = row[:1]
    hi, lo = split(ms_ref[...])
    hi, lo = split(mm(hi, hot_ref[...]) + mm(lo, hot_ref[...]))
    mc_ref[...] = mm(hi, front_ref[...]) + mm(lo, front_ref[...])


def trace_kernel(me_ref, *refs):
    xs = refs[:NF]
    hi_ref, lo_ref, fwd_ref, mc_ref = refs[NF : NF + 4]
    outs = refs[NF + 4 : 2 * NF + 4]
    f_ref, x_ref, r_ref = refs[2 * NF + 4 :]
    me = me_ref[0]
    n = pl.program_id(0)

    @pl.when(n == 0)
    def _():
        fh, fl = split(fwd_ref[...])
        f_ref[:CF] = fh
        f_ref[CF:] = fl

    for k in range(NF):
        j = lax.rem(me - k + NF, NF)
        x_ref[pl.ds(pl.multiple_of(j * ROWS, 8), ROWS), :] = xs[k][0]
    cells = x_ref.shape[1]
    width = min(MAIN, cells)
    t = lax.broadcasted_iota(jnp.int32, (HALF, width), 0).astype(F32)
    for w in range(cells // width):
        at = slice(w * width, (w + 1) * width)
        live = mc_ref[NSH : NSH + 1, at]
        xh, xl = split(jnp.where(live > 0.5, x_ref[:, at], 0.0))
        table = hi_ref[0]
        u = mm(table, xh) + mm(lo_ref[0], xh) + mm(table, xl)
        cut = mc_ref[pl.ds(n, 1), at]
        yh, yl = split(jnp.where(t >= cut, u[:HALF], 0.0))
        p = mm(f_ref[...], yh)
        r_ref[:, at] = u[HALF:] + p[:CF] + p[CF:] + mm(f_ref[:CF], yl)
    for k in range(NF):
        j = lax.rem(me + k, NF)
        outs[k][0] = r_ref[pl.ds(pl.multiple_of(j * ROWS, 8), ROWS), :]


def finish_kernel(at_ref, z_ref, hot_ref, back_ref, rest_ref, *refs):
    rs, out_ref = refs[:NF], refs[NF]
    zv_ref, b_ref, s_ref, t_ref, h_ref, r_sem, q_sem, b_sem, z_sem, out_sem = refs[NF + 1 :]
    me, more = at_ref[0], at_ref[1] > 0
    cells = t_ref.shape[2]
    slots = hot_ref.shape[0]
    tiles = SLABS // 4
    rows = 4 * CF

    def rest_in(k):
        j = lax.rem(me - k + NF, NF)
        to = s_ref.at[pl.ds(j * NSH, NSH), :, MAIN:]
        return pltpu.make_async_copy(rest_ref.at[k], to, q_sem.at[k])

    r_in = []
    for k in range(NF):
        j = lax.rem(me - k + NF, NF)
        to = s_ref.at[pl.ds(j * NSH, NSH), :, :MAIN]
        r_in.append(pltpu.make_async_copy(rs[k], to, r_sem.at[k]))
        r_in[k].start()

    @pl.when(more)
    def _():
        for k in range(NF):
            rest_in(k).start()

    z_in = []
    for tile in range(tiles):
        at = slice(4 * tile, 4 * tile + 4)
        z_in.append(pltpu.make_async_copy(z_ref.at[at], zv_ref.at[at], z_sem.at[tile]))
        z_in[tile].start()
    hot_in = pltpu.make_async_copy(hot_ref, b_ref.at[:slots], b_sem.at[0])
    hot_in.start()
    back_in = pltpu.make_async_copy(back_ref, b_ref.at[slots:], b_sem.at[1])
    back_in.start()
    for load in r_in:
        load.wait()
    for o in range(2):
        at = slice(16 * o, 16 * o + 16)
        hi, lo = split(jnp.swapaxes(s_ref[at, :, :MAIN], 0, 1))
        h_ref[:ROWS, at, slots : slots + MAIN] = hi
        h_ref[ROWS:, at, slots : slots + MAIN] = lo

    @pl.when(more)
    def _():
        for k in range(NF):
            rest_in(k).wait()
        for o in range(2):
            at = slice(16 * o, 16 * o + 16)
            hi, lo = split(jnp.swapaxes(s_ref[at, :, MAIN:], 0, 1))
            h_ref[:ROWS, at, slots + MAIN :] = hi
            h_ref[ROWS:, at, slots + MAIN :] = lo

    lane = lax.broadcasted_iota(jnp.int32, (CF, 128), 1) // SLOT
    each = ROWS // 4
    for tile in range(tiles):
        z_in[tile].wait()
        parts = [zv_ref[4 * tile + e] for e in range(4)]
        at = slice(tile * 128, (tile + 1) * 128)
        for g in range(4):
            hi, lo = split(-regroup(parts, g, lane))
            h_ref[g * each : (g + 1) * each, :, at] = hi.reshape(each, NSH * NF, 128)
            h_ref[ROWS + g * each : ROWS + (g + 1) * each, :, at] = lo.reshape(each, NSH * NF, 128)
    hot_in.wait()
    back_in.wait()
    stores = []
    for w in range(cells // WIDTH):
        at = slice(w * WIDTH, (w + 1) * WIDTH)
        main = h_ref[:, :, : slots + MAIN].reshape(2 * rows, slots + MAIN)
        p = mm(main, b_ref[: slots + MAIN, at])
        t_ref[:, :, at] = (p[:rows] + p[rows:]).reshape(ROWS, NSH * NF, WIDTH)

        @pl.when(more)
        def _():
            extra = h_ref[:, :, slots + MAIN :].reshape(2 * rows, cells - MAIN)
            p = mm(extra, b_ref[slots + MAIN :, at])
            t_ref[:, :, at] = t_ref[:, :, at] + (p[:rows] + p[rows:]).reshape(ROWS, NSH * NF, WIDTH)

        stores.append(pltpu.make_async_copy(t_ref.at[:, :, at], out_ref.at[:, :, at], out_sem.at[w]))
        stores[w].start()
    for store in stores:
        store.wait()


def shift_by(values, k):
    return lax.ppermute(values, "freq", [(i, (i + k) % NF) for i in range(NF)])


def on_device(wavefield, observed, filters, mute, send_cell, send_count, recv_pos):
    cells = wavefield.shape[3]
    group = observed.shape[3]
    slots = send_cell.shape[1]
    me = lax.axis_index("freq").astype(jnp.int32).reshape(1)

    (mute_slots,) = call(mute_kernel, [sds(SLABS, 8, 128)], 2)(recv_pos, mute)
    mute_all = lax.all_to_all(mute_slots, "slab", split_axis=0, concat_axis=0, tiled=True)
    obs = observed.reshape(2, NF, FB, NSH, group)
    own = [
        lax.dynamic_index_in_dim(obs, lax.rem(me[0] + NF - k, NF), 1, keepdims=False).reshape(
            ROWS, NSH, group
        )
        for k in range(NF)
    ]
    own = [own[0]] + [shift_by(own[k], NF - k) for k in range(1, NF)]
    forward = jnp.asarray(forward_table())
    taps = jnp.concatenate([filters[:, ::-1], jnp.zeros_like(filters)], axis=1)
    hi, lo = call(
        operator_kernel,
        [sds(NSH, HALF + CF, CF, dtype=BF)] * 2,
        2,
        scratch=[pltpu.VMEM((CF, NT), BF), pltpu.VMEM((CF, NT), BF), pltpu.VMEM((HALF, CF), F32)],
    )(taps, forward)
    live = jnp.arange(SLOT, dtype=jnp.int32)[None, :] < send_count[0][:, None]
    target = jnp.where(live.reshape(-1), send_cell[0], -1).reshape(slots, 1)
    hot, front, back = call(
        index_kernel,
        [sds(slots, cells, dtype=BF), sds(cells, cells, dtype=BF), sds(cells, cells, dtype=BF)],
        1,
        vmem=60 << 20,
    )(target)
    *blocks, rest = call(
        route_kernel,
        [sds(NSH, ROWS, MAIN)] * NF + [sds(NF, NSH, ROWS, cells - MAIN)],
        3,
        smem=(0,),
        scratch=[
            pltpu.VMEM((NSH * NF, ROWS, cells), F32),
            pltpu.VMEM((2 * ROWS * NSH * NF, cells), BF),
        ],
        vmem=60 << 20,
    )(me, wavefield.reshape(ROWS, NSH * NF, cells), front)
    own, blocks, rest = lax.optimization_barrier((own, blocks, rest))
    (packed,) = call(
        pack_kernel,
        [sds(SLABS, CF, 128)],
        NF + 2,
        smem=(0,),
        scratch=[
            pltpu.VMEM((ROWS, NSH * NF, group), F32),
            pltpu.VMEM((8 * CF, group), BF),
        ],
    )(me, recv_pos, *own)
    arrived = lax.all_to_all(packed, "slab", split_axis=0, concat_axis=0, tiled=True)


    (at_columns,) = call(
        place_kernel,
        [sds(2 * NSH, cells)],
        3,
        scratch=[pltpu.VMEM((2 * NSH, slots), F32)],
    )(mute_all, hot, front)

    def exchanged(blocks):
        return [blocks[0]] + [shift_by(blocks[k], k) for k in range(1, NF)]

    def traced(blocks, hi, lo, forward, columns):
        width = columns.shape[1]
        block = pl.BlockSpec((1, ROWS, width), lambda n: (n, 0, 0))
        table = pl.BlockSpec((1, HALF + CF, CF), lambda n: (n, 0, 0))
        return grid_call(
            trace_kernel,
            [sds(NSH, ROWS, width)] * NF,
            [INS]
            + [block] * NF
            + [table] * 2
            + [
                pl.BlockSpec((CF, HALF), lambda n: (0, 0)),
                pl.BlockSpec((2 * NSH, width), lambda n: (0, 0)),
            ],
            [block] * NF,
            [
                pltpu.VMEM((2 * CF, HALF), BF),
                pltpu.VMEM((CF, width), F32),
                pltpu.VMEM((CF, width), F32),
            ],
        )(me, *exchanged(blocks), hi, lo, forward, columns)

    def traced_rest(rest, hi, lo, forward, columns):
        parts = [rest[k] for k in range(NF)]
        return jnp.stack(exchanged(traced(parts, hi, lo, forward, columns)))

    main = traced(blocks, hi, lo, forward, at_columns[:, :MAIN])
    main, rest = lax.optimization_barrier((main, rest))
    returned = exchanged(main)
    more = jnp.sum(send_count) > MAIN
    rest = lax.cond(
        more,
        traced_rest,
        lambda rest, *_: rest,
        rest,
        hi,
        lo,
        forward,
        at_columns[:, MAIN:],
    )
    dma = pltpu.SemaphoreType.DMA
    (out,) = copy_call(
        finish_kernel,
        [sds(ROWS, NSH * NF, cells)],
        [INS] + [HBM] * (NF + 4),
        [
            pltpu.VMEM((SLABS, CF, 128), F32),
            pltpu.VMEM((slots + cells, cells), BF),
            pltpu.VMEM((NSH * NF, ROWS, cells), F32),
            pltpu.VMEM((ROWS, NSH * NF, cells), F32),
            pltpu.VMEM((2 * ROWS, NSH * NF, slots + cells), BF),
            dma((NF,)),
            dma((NF,)),
            dma((2,)),
            dma((SLABS // 4,)),
            dma((cells // WIDTH,)),
        ],
    )(jnp.concatenate([me, more.astype(jnp.int32).reshape(1)]), arrived, hot, back, rest, *returned)
    return out.reshape(2, FB, NSH * NF, cells)


def solution(mesh):
    return jax.shard_map(
        on_device,
        mesh=mesh,
        in_specs=(
            P(None, "freq", None, "slab"),
            P(None, None, "freq", "slab"),
            P("freq", None),
            P("freq", "slab"),
            P("slab", None),
            P("slab", None),
            P("slab", None),
        ),
        out_specs=P(None, "freq", None, "slab"),
        check_vma=False,
    )
```

```python
import math

import jax
import jax.numpy as jnp
import numpy as np
from jax import lax
from jax.experimental import pallas as pl
from jax.experimental.pallas import tpu as pltpu
from jax.sharding import PartitionSpec as P

F = 96
NT = 1024
TAPS = 256
K0 = 8
HALF = 512
NF = 8
FB = F // NF
ROWS = 2 * FB
CF = 2 * F
SLABS = 32
SLOT = 32
MAIN = 768
NSH = 4
VMEM = 28 << 20
COST = pl.CostEstimate(flops=1000, bytes_accessed=1000, transcendentals=0)
WIDTH = 512
WIDE = 1024
NARROW = 256
HBM = pl.BlockSpec(memory_space=pltpu.HBM)
INV = pl.BlockSpec(memory_space=pltpu.VMEM)
INS = pl.BlockSpec(memory_space=pltpu.SMEM)
BF = jnp.bfloat16
F32 = jnp.float32


def split(x):
    hi = x.astype(BF)
    return hi, (x - hi.astype(F32)).astype(BF)


def mm(a, b):
    return jnp.dot(a, b, preferred_element_type=F32)


def regroup(parts, at, lane):
    acc = None
    for m in range(4):
        shift = (m - at) % 4 * SLOT
        v = pltpu.roll(parts[m], shift, parts[m].ndim - 1) if shift else parts[m]
        acc = v if acc is None else jnp.where(lane == m, v, acc)
    return acc


def mt(a, b):
    return lax.dot_general(a, b, (((1,), (1,)), ((), ())), preferred_element_type=F32)


def call(kernel, outs, n_in, *, smem=(), scratch=(), vmem=VMEM):
    specs = [
        pl.BlockSpec(memory_space=pltpu.SMEM if i in smem else pltpu.VMEM) for i in range(n_in)
    ]
    vm = pl.BlockSpec(memory_space=pltpu.VMEM)
    return pl.pallas_call(
        kernel,
        out_shape=outs,
        in_specs=specs,
        out_specs=[vm] * len(outs),
        scratch_shapes=list(scratch),
        compiler_params=pltpu.CompilerParams(vmem_limit_bytes=vmem),
        cost_estimate=COST,
    )


def copy_call(kernel, outs, in_specs, scratch, vmem=60 << 20):
    return pl.pallas_call(
        kernel,
        out_shape=outs,
        in_specs=in_specs,
        out_specs=[HBM] * len(outs),
        scratch_shapes=list(scratch),
        compiler_params=pltpu.CompilerParams(vmem_limit_bytes=vmem),
        cost_estimate=COST,
    )


def grid_call(kernel, outs, in_specs, out_specs, scratch):
    return pl.pallas_call(
        kernel,
        grid=(4,),
        out_shape=outs,
        in_specs=in_specs,
        out_specs=out_specs,
        scratch_shapes=list(scratch),
        compiler_params=pltpu.CompilerParams(vmem_limit_bytes=VMEM),
        cost_estimate=COST,
    )


def sds(*shape, dtype=F32):
    return jax.ShapeDtypeStruct(shape, dtype)


def forward_table():
    row = np.arange(CF)
    part = (row % ROWS) // FB
    freq = K0 + (row // ROWS) * FB + row % FB
    angle = (freq[:, None] * np.arange(NT)[None, :] % NT) * (2.0 * math.pi / NT)
    wave = np.where(part[:, None] == 0, np.cos(angle), -np.sin(angle))
    return (wave / math.sqrt(NT)).astype(np.float32)


def operator_kernel(taps_ref, fwd_ref, hi_ref, lo_ref, ih_ref, il_ref, g_ref):
    ih, il = split(fwd_ref[...] * math.sqrt(NT / F))
    ih_ref[...] = ih
    il_ref[...] = il
    late = split(fwd_ref[:, HALF:])

    @pl.loop(0, NSH)
    def _(n):
        rows = jnp.broadcast_to(taps_ref[pl.ds(n, 1), :], (TAPS, 2 * TAPS))
        bh, bl = split(pltpu.roll(rows, 1, 1, stride=1, stride_axis=0))
        for b in range(NT // TAPS):
            at = slice(max(b - 1, 0) * TAPS, (b + 1) * TAPS)
            taps = slice(TAPS if b == 0 else 0, 2 * TAPS)
            g = mt(bh[:, taps], ih_ref[:, at]) + mt(bh[:, taps], il_ref[:, at])
            g = g + mt(bl[:, taps], ih_ref[:, at])
            if b < 2:
                hi, lo = split(g)
                hi_ref[n, b * TAPS : (b + 1) * TAPS, :] = hi
                lo_ref[n, b * TAPS : (b + 1) * TAPS, :] = lo
            else:
                g_ref[(b - 2) * TAPS : (b - 1) * TAPS, :] = g
        gh, gl = split(g_ref[...])
        hi, lo = split(mm(late[0], gh) + mm(late[0], gl) + mm(late[1], gh))
        hi_ref[n, HALF:, :] = hi
        lo_ref[n, HALF:, :] = lo


def mute_kernel(pos_ref, mute_ref, out_ref):
    group = mute_ref.shape[1]
    slots = pos_ref.shape[1]
    pick = (
        lax.broadcasted_iota(jnp.int32, (group, slots), 0) == jnp.broadcast_to(pos_ref[...], (group, slots))
    ).astype(F32).astype(BF)
    mh, ml = split(mute_ref[...].astype(F32))
    got = mm(mh, pick) + mm(ml, pick)
    lane = lax.broadcasted_iota(jnp.int32, (8, 128), 1) // SLOT
    for tile in range(SLABS // 4):
        rows = [
            jnp.broadcast_to(got[n : n + 1, tile * 128 : (tile + 1) * 128], (8, 128))
            for n in range(NSH)
        ]
        for b in range(4):
            out_ref[4 * tile + b] = regroup(rows, b, lane)


def pack_kernel(me_ref, pos_ref, *refs):
    blocks = refs[:NF]
    out_ref, x_ref, h_ref = refs[NF:]
    me = me_ref[0]
    group = x_ref.shape[2]
    slots = pos_ref.shape[1]
    rows = 4 * CF
    for k in range(NF):
        x_ref[:, k * NSH : (k + 1) * NSH, :] = blocks[k][...]
    x = pltpu.roll(x_ref[...], me * NSH, 1).reshape(rows, group)
    h_ref[:rows], h_ref[rows:] = split(x)
    lane = lax.broadcasted_iota(jnp.int32, (CF, 128), 1) // SLOT
    for w in range(slots // WIDTH):
        at = slice(w * WIDTH, (w + 1) * WIDTH)
        pick = (
            lax.broadcasted_iota(jnp.int32, (group, WIDTH), 0)
            == jnp.broadcast_to(pos_ref[:, at], (group, WIDTH))
        ).astype(F32).astype(BF)
        y = mm(h_ref[...], pick)
        y = y[:rows] + y[rows:]
        for i in range(WIDTH // 128):
            tile = w * (WIDTH // 128) + i
            parts = [y[g * CF : (g + 1) * CF, i * 128 : (i + 1) * 128] for g in range(4)]
            for b in range(4):
                out_ref[4 * tile + b] = regroup(parts, b, lane)


def index_kernel(cell_ref, hot_ref, front_ref, back_ref):
    slots, cells = hot_ref.shape
    hot = (
        lax.broadcasted_iota(jnp.int32, (slots, cells), 1) == jnp.broadcast_to(cell_ref[...], (slots, cells))
    ).astype(F32).astype(BF)
    hot_ref[...] = hot
    live = mm(jnp.ones((8, slots), BF), hot)
    before = (
        lax.broadcasted_iota(jnp.int32, (cells, cells), 0) < lax.broadcasted_iota(jnp.int32, (cells, cells), 1)
    ).astype(F32).astype(BF)
    rank = mm(live.astype(BF), before)
    place = jnp.where(live > 0.5, rank, -1.0)[:1]
    back = (
        lax.broadcasted_iota(jnp.int32, (cells, cells), 0).astype(F32) == jnp.broadcast_to(place, (cells, cells))
    ).astype(F32)
    back_ref[...] = back.astype(BF)
    front_ref[...] = jnp.transpose(back).astype(BF)


def route_kernel(me_ref, x_ref, front_ref, *refs):
    outs, rest_ref, st_ref, h_ref = refs[:NF], refs[NF], refs[NF + 1], refs[NF + 2]
    rows, cells = ROWS * NSH * NF, x_ref.shape[2]
    h_ref[:rows], h_ref[rows:] = split(x_ref[...].reshape(rows, cells))

    @pl.loop(0, cells // WIDE)
    def _(w):
        at = pl.ds(pl.multiple_of(w * WIDE, WIDE), WIDE)
        y = mm(h_ref[...], front_ref[:, at])
        y = (y[:rows] + y[rows:]).reshape(ROWS, NSH * NF, WIDE)
        for o in range(4):
            st_ref[8 * o : 8 * o + 8, :, at] = jnp.swapaxes(y[:, 8 * o : 8 * o + 8, :], 0, 1)
    me = me_ref[0]
    for k in range(NF):
        j = lax.rem(me + k, NF)
        outs[k][...] = st_ref[pl.ds(j * NSH, NSH), :, :MAIN]
        rest_ref[k] = st_ref[pl.ds(j * NSH, NSH), :, MAIN:]


def place_kernel(all_ref, hot_ref, front_ref, mc_ref, ms_ref):
    lane = lax.broadcasted_iota(jnp.int32, (8, 128), 1) // SLOT
    ms_ref[...] = jnp.ones_like(ms_ref)
    for tile in range(SLABS // 4):
        for n in range(NSH):
            row = regroup([all_ref[4 * tile + e] for e in range(4)], n, lane)
            ms_ref[n : n + 1, tile * 128 : (tile + 1) * 128] = row[:1]
    hi, lo = split(ms_ref[...])
    hi, lo = split(mm(hi, hot_ref[...]) + mm(lo, hot_ref[...]))
    mc_ref[...] = mm(hi, front_ref[...]) + mm(lo, front_ref[...])


def trace_kernel(me_ref, *refs):
    xs = refs[:NF]
    hi_ref, lo_ref, fwd_ref, mc_ref = refs[NF : NF + 4]
    outs = refs[NF + 4 : 2 * NF + 4]
    f_ref, x_ref, r_ref = refs[2 * NF + 4 :]
    me = me_ref[0]
    n = pl.program_id(0)

    @pl.when(n == 0)
    def _():
        fh, fl = split(fwd_ref[...])
        f_ref[:CF] = fh
        f_ref[CF:] = fl

    for k in range(NF):
        j = lax.rem(me - k + NF, NF)
        x_ref[pl.ds(pl.multiple_of(j * ROWS, 8), ROWS), :] = xs[k][0]
    cells = x_ref.shape[1]
    width = min(MAIN, cells)
    t = lax.broadcasted_iota(jnp.int32, (HALF, width), 0).astype(F32)
    for w in range(cells // width):
        at = slice(w * width, (w + 1) * width)
        live = mc_ref[NSH : NSH + 1, at]
        xh, xl = split(jnp.where(live > 0.5, x_ref[:, at], 0.0))
        table = hi_ref[0]
        u = mm(table, xh) + mm(lo_ref[0], xh) + mm(table, xl)
        cut = mc_ref[pl.ds(n, 1), at]
        yh, yl = split(jnp.where(t >= cut, u[:HALF], 0.0))
        p = mm(f_ref[...], yh)
        r_ref[:, at] = u[HALF:] + p[:CF] + p[CF:] + mm(f_ref[:CF], yl)
    for k in range(NF):
        j = lax.rem(me + k, NF)
        outs[k][0] = r_ref[pl.ds(pl.multiple_of(j * ROWS, 8), ROWS), :]


def finish_kernel(at_ref, z_ref, hot_ref, back_ref, rest_ref, *refs):
    rs, out_ref = refs[:NF], refs[NF]
    zv_ref, b_ref, s_ref, t_ref, h_ref, r_sem, q_sem, b_sem, z_sem, out_sem = refs[NF + 1 :]
    me, more = at_ref[0], at_ref[1] > 0
    cells = t_ref.shape[2]
    slots = hot_ref.shape[0]
    tiles = SLABS // 4
    rows = 4 * CF

    def rest_in(k):
        j = lax.rem(me - k + NF, NF)
        to = s_ref.at[pl.ds(j * NSH, NSH), :, MAIN:]
        return pltpu.make_async_copy(rest_ref.at[k], to, q_sem.at[k])

    r_in = []
    for k in range(NF):
        j = lax.rem(me - k + NF, NF)
        to = s_ref.at[pl.ds(j * NSH, NSH), :, :MAIN]
        r_in.append(pltpu.make_async_copy(rs[k], to, r_sem.at[k]))
        r_in[k].start()

    @pl.when(more)
    def _():
        for k in range(NF):
            rest_in(k).start()

    z_in = []
    for tile in range(tiles):
        at = slice(4 * tile, 4 * tile + 4)
        z_in.append(pltpu.make_async_copy(z_ref.at[at], zv_ref.at[at], z_sem.at[tile]))
        z_in[tile].start()
    hot_in = pltpu.make_async_copy(hot_ref, b_ref.at[:slots], b_sem.at[0])
    hot_in.start()
    back_in = pltpu.make_async_copy(back_ref, b_ref.at[slots:], b_sem.at[1])
    back_in.start()
    for load in r_in:
        load.wait()
    for o in range(2):
        at = slice(16 * o, 16 * o + 16)
        hi, lo = split(jnp.swapaxes(s_ref[at, :, :MAIN], 0, 1))
        h_ref[:ROWS, at, slots : slots + MAIN] = hi
        h_ref[ROWS:, at, slots : slots + MAIN] = lo

    @pl.when(more)
    def _():
        for k in range(NF):
            rest_in(k).wait()
        for o in range(2):
            at = slice(16 * o, 16 * o + 16)
            hi, lo = split(jnp.swapaxes(s_ref[at, :, MAIN:], 0, 1))
            h_ref[:ROWS, at, slots + MAIN :] = hi
            h_ref[ROWS:, at, slots + MAIN :] = lo

    lane = lax.broadcasted_iota(jnp.int32, (CF, 128), 1) // SLOT
    each = ROWS // 4
    for tile in range(tiles):
        z_in[tile].wait()
        parts = [zv_ref[4 * tile + e] for e in range(4)]
        at = slice(tile * 128, (tile + 1) * 128)
        for g in range(4):
            hi, lo = split(-regroup(parts, g, lane))
            h_ref[g * each : (g + 1) * each, :, at] = hi.reshape(each, NSH * NF, 128)
            h_ref[ROWS + g * each : ROWS + (g + 1) * each, :, at] = lo.reshape(each, NSH * NF, 128)
    hot_in.wait()
    back_in.wait()
    stores = []
    for w in range(cells // NARROW):
        at = slice(w * NARROW, (w + 1) * NARROW)
        main = h_ref[:, :, : slots + MAIN].reshape(2 * rows, slots + MAIN)
        p = mm(main, b_ref[: slots + MAIN, at])
        t_ref[:, :, at] = (p[:rows] + p[rows:]).reshape(ROWS, NSH * NF, NARROW)

        @pl.when(more)
        def _():
            extra = h_ref[:, :, slots + MAIN :].reshape(2 * rows, cells - MAIN)
            p = mm(extra, b_ref[slots + MAIN :, at])
            t_ref[:, :, at] = t_ref[:, :, at] + (p[:rows] + p[rows:]).reshape(ROWS, NSH * NF, NARROW)

        stores.append(pltpu.make_async_copy(t_ref.at[:, :, at], out_ref.at[:, :, at], out_sem.at[w]))
        stores[w].start()
    for store in stores:
        store.wait()


def shift_by(values, k):
    return lax.ppermute(values, "freq", [(i, (i + k) % NF) for i in range(NF)])


def on_device(wavefield, observed, filters, mute, send_cell, send_count, recv_pos):
    cells = wavefield.shape[3]
    group = observed.shape[3]
    slots = send_cell.shape[1]
    me = lax.axis_index("freq").astype(jnp.int32).reshape(1)

    (mute_slots,) = call(mute_kernel, [sds(SLABS, 8, 128)], 2)(recv_pos, mute)
    mute_all = lax.all_to_all(mute_slots, "slab", split_axis=0, concat_axis=0, tiled=True)
    obs = observed.reshape(2, NF, FB, NSH, group)
    own = [
        lax.dynamic_index_in_dim(obs, lax.rem(me[0] + NF - k, NF), 1, keepdims=False).reshape(
            ROWS, NSH, group
        )
        for k in range(NF)
    ]
    own = [own[0]] + [shift_by(own[k], NF - k) for k in range(1, NF)]
    forward = jnp.asarray(forward_table())
    taps = jnp.concatenate([filters[:, ::-1], jnp.zeros_like(filters)], axis=1)
    hi, lo = call(
        operator_kernel,
        [sds(NSH, HALF + CF, CF, dtype=BF)] * 2,
        2,
        scratch=[pltpu.VMEM((CF, NT), BF), pltpu.VMEM((CF, NT), BF), pltpu.VMEM((HALF, CF), F32)],
    )(taps, forward)
    live = jnp.arange(SLOT, dtype=jnp.int32)[None, :] < send_count[0][:, None]
    target = jnp.where(live.reshape(-1), send_cell[0], -1).reshape(slots, 1)
    hot, front, back = call(
        index_kernel,
        [sds(slots, cells, dtype=BF), sds(cells, cells, dtype=BF), sds(cells, cells, dtype=BF)],
        1,
        vmem=60 << 20,
    )(target)
    *blocks, rest = call(
        route_kernel,
        [sds(NSH, ROWS, MAIN)] * NF + [sds(NF, NSH, ROWS, cells - MAIN)],
        3,
        smem=(0,),
        scratch=[
            pltpu.VMEM((NSH * NF, ROWS, cells), F32),
            pltpu.VMEM((2 * ROWS * NSH * NF, cells), BF),
        ],
        vmem=60 << 20,
    )(me, wavefield.reshape(ROWS, NSH * NF, cells), front)
    own, blocks, rest = lax.optimization_barrier((own, blocks, rest))
    (packed,) = call(
        pack_kernel,
        [sds(SLABS, CF, 128)],
        NF + 2,
        smem=(0,),
        scratch=[
            pltpu.VMEM((ROWS, NSH * NF, group), F32),
            pltpu.VMEM((8 * CF, group), BF),
        ],
    )(me, recv_pos, *own)
    arrived = lax.all_to_all(packed, "slab", split_axis=0, concat_axis=0, tiled=True)


    (at_columns,) = call(
        place_kernel,
        [sds(2 * NSH, cells)],
        3,
        scratch=[pltpu.VMEM((2 * NSH, slots), F32)],
    )(mute_all, hot, front)

    def exchanged(blocks):
        return [blocks[0]] + [shift_by(blocks[k], k) for k in range(1, NF)]

    def traced(blocks, hi, lo, forward, columns):
        width = columns.shape[1]
        block = pl.BlockSpec((1, ROWS, width), lambda n: (n, 0, 0))
        table = pl.BlockSpec((1, HALF + CF, CF), lambda n: (n, 0, 0))
        return grid_call(
            trace_kernel,
            [sds(NSH, ROWS, width)] * NF,
            [INS]
            + [block] * NF
            + [table] * 2
            + [
                pl.BlockSpec((CF, HALF), lambda n: (0, 0)),
                pl.BlockSpec((2 * NSH, width), lambda n: (0, 0)),
            ],
            [block] * NF,
            [
                pltpu.VMEM((2 * CF, HALF), BF),
                pltpu.VMEM((CF, width), F32),
                pltpu.VMEM((CF, width), F32),
            ],
        )(me, *exchanged(blocks), hi, lo, forward, columns)

    def traced_rest(rest, hi, lo, forward, columns):
        parts = [rest[k] for k in range(NF)]
        return jnp.stack(exchanged(traced(parts, hi, lo, forward, columns)))

    main = traced(blocks, hi, lo, forward, at_columns[:, :MAIN])
    main, rest = lax.optimization_barrier((main, rest))
    returned = exchanged(main)
    more = jnp.sum(send_count) > MAIN
    rest = lax.cond(
        more,
        traced_rest,
        lambda rest, *_: rest,
        rest,
        hi,
        lo,
        forward,
        at_columns[:, MAIN:],
    )
    dma = pltpu.SemaphoreType.DMA
    (out,) = copy_call(
        finish_kernel,
        [sds(ROWS, NSH * NF, cells)],
        [INS] + [HBM] * (NF + 4),
        [
            pltpu.VMEM((SLABS, CF, 128), F32),
            pltpu.VMEM((slots + cells, cells), BF),
            pltpu.VMEM((NSH * NF, ROWS, cells), F32),
            pltpu.VMEM((ROWS, NSH * NF, cells), F32),
            pltpu.VMEM((2 * ROWS, NSH * NF, slots + cells), BF),
            dma((NF,)),
            dma((NF,)),
            dma((2,)),
            dma((SLABS // 4,)),
            dma((cells // NARROW,)),
        ],
    )(jnp.concatenate([me, more.astype(jnp.int32).reshape(1)]), arrived, hot, back, rest, *returned)
    return out.reshape(2, FB, NSH * NF, cells)


def solution(mesh):
    return jax.shard_map(
        on_device,
        mesh=mesh,
        in_specs=(
            P(None, "freq", None, "slab"),
            P(None, None, "freq", "slab"),
            P("freq", None),
            P("freq", "slab"),
            P("slab", None),
            P("slab", None),
            P("slab", None),
        ),
        out_specs=P(None, "freq", None, "slab"),
        check_vma=False,
    )
```
